512 devices in a mesh: energy: 64 (over z, y), space: 8 (over x, core).
Axes of the slice: x: 4, y: 8, z: 8, core: 2. Of those that a mesh axis runs over, the one named last changes fastest.
Arguments:
- green_ret: bfloat16 [64, 64, 128, 128], P('energy', 'space'), may hold values from -0.5 to 0.5
- prior_less: bfloat16 [64, 64, 128, 128], P('energy', 'space'), may hold values from -1.25 to 9.25
- prior_great: bfloat16 [64, 64, 128, 128], P('energy', 'space'), may hold values from -1.25 to 9.25
- coupling: bfloat16 [64, 128, 128], P('space'), may hold values from -0.5 to 0.5
- phonon_coupling: float32 [128, 128], P('energy'), may hold values from 0.1 to 1
- phonon_shift: int32 [2], replicated, may hold values from 1 to 32
- active_blocks: int32 [64], replicated, may hold values from 32 to 64
Outputs:
- sigma_less: bfloat16 [64, 64, 128, 128], P(None, 'space', 'energy')
- sigma_great: bfloat16 [64, 64, 128, 128], P(None, 'space', 'energy')
- current: float32 [64, 64], P('energy', 'space')
- ldos: float32 [64, 64], P('energy', 'space')
The draws below stay inside these ranges and needn't reach their ends.
All inputs are finite; a program needn't handle non-finite values.
Results may differ from the reference program's by a relative error of at most 0.009.
Values may be sent and summed in bfloat16 or wider, within the bound.
A program may use at most 64 MiB of HBM per device.

```python
import math
import jax
import jax.numpy as jnp
from jax import lax

B = 128
NE = 64
NB = 64


def prior_block(key):
    first, second = jax.random.split(key)
    noise = jnp.clip(0.3 * jax.random.normal(first, (NE, NB, B, B), jnp.float32), -1.2, 1.2)
    diagonal = jnp.exp(jax.random.uniform(second, (NE, NB, B, 1), jnp.float32, math.log(0.5), math.log(4.0)))
    identity = jnp.eye(B, dtype=jnp.float32)
    return noise + identity * diagonal


def draw_prior_less(key, part):
    return prior_block(jax.random.fold_in(key, 11)).astype(jnp.bfloat16)


def draw_prior_great(key, part):
    return prior_block(jax.random.fold_in(key, 23)).astype(jnp.bfloat16)


def plant(drawn, own_key, low, high):
    place = [jax.random.randint(jax.random.fold_in(own_key, axis), (), 0, length) for axis, length in enumerate(drawn.shape)]
    widest = drawn.shape.index(max(drawn.shape))
    beside = place[:widest] + [(place[widest] + 1) % drawn.shape[widest]] + place[widest + 1:]
    return drawn.at[tuple(place)].set(low).at[tuple(beside)].set(high)


def shard_levels(key, extent, cuts, low, high):
    gain, own = 1.0, jax.random.fold_in(key, 6)
    for dim, blocks in cuts:
        draws = jnp.exp(jax.random.uniform(jax.random.fold_in(own, dim), (blocks,), jnp.float32, low / len(cuts), high / len(cuts)))
        gain = gain * jnp.repeat(draws, extent[dim] // blocks).reshape([-1 if axis == dim else 1 for axis in range(len(extent))])
    return gain


def centred(own_key, shape, width, bound, cuts=(), kind=jnp.bfloat16):
    array = width * jax.random.normal(own_key, shape, jnp.float32)
    if cuts:
        array = array * shard_levels(own_key, shape, cuts, -0.22, 0.18)
    return jnp.clip(array, -bound, bound).astype(kind)


def setup_inputs(seed: int = 0) -> dict:
    seeds = jax.random.split(jax.random.key(seed), 8)
    return {
        "green_ret": centred(seeds[0], (NE, NB, B, B), B ** -0.5, 0.5, ((0, 64), (1, 8))),
        "prior_less": draw_prior_less(jax.random.fold_in(seeds[7], 71), 0),
        "prior_great": draw_prior_great(jax.random.fold_in(seeds[7], 71), 0),
        "coupling": centred(seeds[3], (NB, B, B), B ** -0.5, 0.5, ((0, 8),)),
        "phonon_coupling": jnp.clip(jnp.exp(math.log(1.0) - 2.3025851 * jax.random.uniform(seeds[4], (B, B), jnp.float32) ** shard_levels(seeds[4], (B, B), ((0, 64),), -0.2, 0.2)), 0.1, 1.0),
        "phonon_shift": jax.random.randint(seeds[5], (2,), 1, NE // 2 + 1).astype(jnp.int32),
        "active_blocks": plant(jax.random.randint(seeds[6], (NE,), NB // 2, NB + 1), jax.random.fold_in(seeds[6], 1), NB // 2, NB).astype(jnp.int32),
    }


phonon_occupation = 0.5


def widen(values):
    return values.astype(jnp.float32)


def propagate(retarded, prior, coupling, open_mask):
    half_product = jnp.einsum("nij,njl->nil", widen(retarded), widen(prior)).astype(jnp.bfloat16)
    bare = jnp.einsum("nil,nml->nim", widen(half_product), widen(retarded)).astype(jnp.bfloat16)
    raised = jnp.einsum("nji,njl->nil", widen(coupling), widen(bare)).astype(jnp.bfloat16)
    upward = jnp.einsum("nil,nlm->nim", widen(raised), widen(coupling)).astype(jnp.bfloat16)
    following = jnp.concatenate([bare[1:], jnp.zeros_like(bare[:1])], 0)
    lowered = jnp.einsum("nij,njl->nil", widen(coupling), widen(following)).astype(jnp.bfloat16)
    downward = jnp.einsum("nil,nml->nim", widen(lowered), widen(coupling))
    previous = jnp.concatenate([jnp.zeros_like(upward[:1]), upward[:-1]], 0)
    source = (widen(prior) + widen(previous) + downward).astype(jnp.bfloat16)
    second_half = jnp.einsum("nij,njl->nil", widen(retarded), widen(source)).astype(jnp.bfloat16)
    result = jnp.einsum("nil,nml->nim", widen(second_half), widen(retarded))
    return (result * open_mask[:, None, None]).astype(jnp.bfloat16)


def at_energy(blocks_in, target):
    inside_grid = (target >= 0) & (target < NE)
    clipped = jnp.clip(target, 0, NE - 1).astype(jnp.int32)
    piece = lax.dynamic_index_in_dim(blocks_in, clipped, 0, keepdims=False)
    return jnp.where(inside_grid, widen(piece), jnp.float32(0.0))


def reference(green_ret, prior_less, prior_great, coupling, phonon_coupling, phonon_shift, active_blocks):
    positions = jnp.arange(NB, dtype=jnp.int32)

    def per_energy(inputs):
        retarded, less_part, great_part, open_count = inputs
        open_mask = (positions < open_count).astype(jnp.float32)
        return (propagate(retarded, less_part, coupling, open_mask),
                propagate(retarded, great_part, coupling, open_mask))

    lesser, greater = lax.map(per_energy, (green_ret, prior_less, prior_great, active_blocks))
    diag_mask = jnp.eye(B, dtype=jnp.float32)
    occupied = jnp.float32(phonon_occupation)

    def per_energy_out(energy_index):
        less_sum = jnp.zeros((NB, B, B), jnp.float32)
        great_sum = jnp.zeros((NB, B, B), jnp.float32)
        for branch in range(2):
            offset = phonon_shift[branch]
            less_up = at_energy(lesser, energy_index + offset)
            less_down = at_energy(lesser, energy_index - offset)
            great_up = at_energy(greater, energy_index + offset)
            great_down = at_energy(greater, energy_index - offset)
            less_sum = less_sum + (1.0 + occupied) * less_up + occupied * less_down
            great_sum = great_sum + (1.0 + occupied) * great_down + occupied * great_up
        sigma_l = (phonon_coupling * less_sum).astype(jnp.bfloat16)
        sigma_g = (phonon_coupling * great_sum).astype(jnp.bfloat16)
        lesser_here = at_energy(lesser, energy_index)
        greater_here = at_energy(greater, energy_index)
        scattering = jnp.sum(widen(sigma_l) * greater_here - widen(sigma_g) * lesser_here, axis=(1, 2)) / B
        density = jnp.sum((lesser_here + greater_here) * diag_mask, axis=(1, 2)) / B
        return sigma_l, sigma_g, scattering, density

    sigma_less, sigma_great, current, ldos = lax.map(per_energy_out, jnp.arange(NE, dtype=jnp.int32))
    return (sigma_less, sigma_great, current, ldos)
```

```python
import functools

import jax
import jax.numpy as jnp
from jax import lax
from jax.experimental import pallas as pl
from jax.experimental.pallas import tpu as pltpu
from jax.sharding import PartitionSpec as P

phonon_occupation = 0.5
MESH = pl.DeviceIdType.MESH
F32 = jnp.float32
BF16 = jnp.bfloat16

NE = 64
NB = 8
NO = 128
HALF = 4
PAD = 32
SIDE = 8


def dot(left, right):
    return jnp.dot(left, right, preferred_element_type=F32)


def dot_t(left, right):
    return lax.dot_general(left, right, (((1,), (1,)), ((), ())), preferred_element_type=F32)


def side_by_side(stacked):
    return jnp.concatenate([stacked[:NO], stacked[NO:]], axis=1)


def stacked(wide):
    return jnp.concatenate([wide[:, :NO], wide[:, NO:]], axis=0)


def kernel(
    g_ref, pl_ref, pg_ref, c_ref, pc_ref, shift_ref, active_ref,
    sl_ref, sg_ref, cur_ref, ldos_ref,
    bare, ct, up_out, up_in, rows, send, recv_low, recv_high, part, total,
    halo_send, halo_recv, x_send, x_recv, t_send, t_recv,
):
    me = lax.axis_index("energy")
    space = lax.axis_index("space")
    spaces = lax.axis_size("space")
    recvs = (recv_low, recv_high)

    barrier = pltpu.get_barrier_semaphore()

    @pl.loop(1, NE)
    def _(k):
        pl.semaphore_signal(barrier, inc=1, device_id={"energy": (me + k) % NE}, device_id_type=MESH)

    @pl.when(space > 0)
    def _():
        pl.semaphore_signal(barrier, inc=1, device_id={"space": space - 1}, device_id_type=MESH)

    @pl.when(space < spaces - 1)
    def _():
        pl.semaphore_signal(barrier, inc=1, device_id={"space": space + 1}, device_id_type=MESH)

    row_id = lax.broadcasted_iota(jnp.int32, (NO, NO), 0)
    col_id = lax.broadcasted_iota(jnp.int32, (NO, NO), 1)
    original = 2 * (row_id % NE) + row_id // NE
    select = col_id == original
    permute = jnp.where(select, F32(1), F32(0)).astype(BF16)
    diagonal = jnp.where(select, F32(1), F32(0))

    def prior(b):
        return jnp.concatenate([pl_ref[b], pg_ref[b]], axis=0)

    def make_bare(b):
        wide = jnp.concatenate([pl_ref[b], pg_ref[b]], axis=1)
        half = dot(g_ref[b], wide).astype(BF16)
        bare[b] = dot_t(stacked(half), g_ref[b]).astype(BF16)

    def rise(b):
        return stacked(dot(ct[b], side_by_side(bare[b])).astype(BF16))

    for g in range(2):
        recvs[g][0:PAD] = jnp.zeros((PAD, 16, NO), BF16)
        recvs[g][PAD + NE :] = jnp.zeros((PAD, 16, NO), BF16)
    for b in range(NB):
        ct[b] = c_ref[b].T

    make_bare(0)
    make_bare(NB - 1)
    up_out[...] = dot(rise(NB - 1), c_ref[NB - 1]).astype(BF16)

    neighbours = (space > 0).astype(jnp.int32) + (space < spaces - 1).astype(jnp.int32)
    pl.semaphore_wait(barrier, NE - 1 + neighbours)

    down_copy = pltpu.make_async_remote_copy(
        src_ref=bare.at[0], dst_ref=bare.at[NB], send_sem=halo_send.at[0], recv_sem=halo_recv.at[0],
        device_id={"space": lax.rem(space + spaces - 1, spaces)}, device_id_type=MESH,
    )
    up_copy = pltpu.make_async_remote_copy(
        src_ref=up_out, dst_ref=up_in, send_sem=halo_send.at[1], recv_sem=halo_recv.at[1],
        device_id={"space": lax.rem(space + 1, spaces)}, device_id_type=MESH,
    )

    @pl.when(space > 0)
    def _():
        down_copy.start()

    @pl.when(space < spaces - 1)
    def _():
        up_copy.start()

    for b in range(1, NB - 1):
        make_bare(b)

    @pl.when(space == 0)
    def _():
        up_in[...] = jnp.zeros_like(up_in)

    @pl.when(space == spaces - 1)
    def _():
        bare[NB] = jnp.zeros((2 * NO, NO), BF16)

    open_count = active_ref[me]
    lane8 = lax.broadcasted_iota(jnp.int32, (8, NO), 1)
    sub8 = lax.broadcasted_iota(jnp.int32, (8, NO), 0)

    def finish(b, ldos):
        fall = stacked(dot(c_ref[b], side_by_side(bare[b + 1])).astype(BF16))
        if b == 0:
            hops = dot(fall, ct[0]) + up_in[...].astype(F32)
        else:
            left = jnp.concatenate([rise(b - 1), fall], axis=1)
            right = jnp.concatenate([c_ref[b - 1], ct[b]], axis=0)
            hops = dot(left, right)
        source = (prior(b).astype(F32) + hops).astype(BF16)
        mine = dot(permute, g_ref[b]).astype(BF16)
        half = dot(mine, side_by_side(source)).astype(BF16)
        result = dot_t(stacked(half), g_ref[b])
        result = result * jnp.where(space * NB + b < open_count, F32(1), F32(0))
        trace = jnp.sum((result[:NO] + result[NO:]) * diagonal, axis=0, keepdims=True)
        g, inside = b // HALF, b % HALF
        for kind in range(2):
            for r in range(2):
                start = kind * 8 + inside * 2 + r
                at = kind * NO + r * NE
                rows[g, pl.ds(start, NE, stride=16), :] = result[at : at + NE]
        return jnp.where(sub8 == b, jnp.broadcast_to(trace, (8, NO)), ldos)

    def exchange(g, k):
        p = (me + k) % NE
        return pltpu.make_async_remote_copy(
            src_ref=send.at[g, p], dst_ref=recvs[g].at[PAD + me], send_sem=x_send.at[g], recv_sem=x_recv.at[g],
            device_id={"energy": p}, device_id_type=MESH,
        )

    def send_half(g):
        send[g] = rows[g].reshape(NE, 16, NO).astype(BF16)

        @pl.loop(1, NE)
        def _(k):
            exchange(g, k).start()

        recvs[g][PAD + me] = send[g, me]

    def whole(g):
        return pltpu.make_async_remote_copy(
            src_ref=send.at[g, pl.ds(0, NE - 1)], dst_ref=recvs[g].at[pl.ds(0, NE - 1)],
            send_sem=x_send.at[g], recv_sem=x_recv.at[g],
            device_id={"energy": (me + 1) % NE}, device_id_type=MESH,
        )

    ldos = jnp.zeros((8, NO), F32)

    @pl.when(space < spaces - 1)
    def _():
        down_copy.wait_recv()

    for b in range(HALF, NB):
        ldos = finish(b, ldos)
    send_half(1)

    @pl.when(space > 0)
    def _():
        up_copy.wait_recv()

    for b in range(HALF):
        ldos = finish(b, ldos)
    send_half(0)

    def as_row(columns):
        sums = jnp.sum(columns, axis=1, keepdims=True)
        return jnp.sum(jnp.where(lane8 == sub8, sums, F32(0)), axis=0, keepdims=True)[:, :NB]

    ldos_ref[...] = as_row(ldos) / NO

    occupied = F32(phonon_occupation)
    coupling8 = jnp.where(sub8 % 2 == 0, pc_ref[0:1, :], pc_ref[1:2, :])
    strong, weak = coupling8 * (1 + occupied), coupling8 * occupied
    s0, s1 = shift_ref[0], shift_ref[1]

    def sigma(g):
        whole(g).wait_recv()
        recv = recvs[g]

        def step(e, acc):
            at = PAD + e
            here = recv[at].astype(F32)
            up = recv[at + s0].astype(F32) + recv[at + s1].astype(F32)
            down = recv[at - s0].astype(F32) + recv[at - s1].astype(F32)
            less = (strong * up[:8] + weak * down[:8]).astype(BF16)
            great = (strong * down[8:] + weak * up[8:]).astype(BF16)
            sl_ref[e, g] = less
            sg_ref[e, g] = great
            flow = less.astype(F32) * here[8:] - great.astype(F32) * here[:8]
            sums = jnp.sum(flow, axis=1, keepdims=True)
            return jnp.where(lane8 == e, sums, acc)

        part[pl.ds(8 * g, 8), :] = lax.fori_loop(0, NE, step, jnp.zeros((8, NO), F32), unroll=8)

    sigma(1)
    sigma(0)

    z, y = me // SIDE, me % SIDE
    value = part[pl.ds(0, 8, stride=2), :] + part[pl.ds(1, 8, stride=2), :]
    for phase in range(2):
        mine = y if phase == 0 else z
        total[phase, mine] = value

        def hop(k, phase=phase, mine=mine):
            there = (mine + k) % SIDE
            peer = z * SIDE + there if phase == 0 else there * SIDE + y
            return pltpu.make_async_remote_copy(
                src_ref=total.at[phase, mine], dst_ref=total.at[phase, mine],
                send_sem=t_send.at[phase], recv_sem=t_recv.at[phase],
                device_id={"energy": peer}, device_id_type=MESH,
            )

        for k in range(1, SIDE):
            hop(k).start()
        everything = pltpu.make_async_remote_copy(
            src_ref=total.at[phase, pl.ds(0, SIDE - 1)], dst_ref=total.at[phase, pl.ds(0, SIDE - 1)],
            send_sem=t_send.at[phase], recv_sem=t_recv.at[phase],
            device_id={"energy": (me + 1) % NE}, device_id_type=MESH,
        )
        everything.wait_recv()
        value = jnp.sum(total[phase], axis=0)
        everything.wait_send()

    cur_ref[...] = as_row(jnp.where(lane8 == me, value, F32(0))) / NO

    @pl.when(space > 0)
    def _():
        down_copy.wait_send()

    @pl.when(space < spaces - 1)
    def _():
        up_copy.wait_send()

    whole(1).wait_send()
    whole(0).wait_send()


def local(
    green_ret, prior_less, prior_great, coupling, phonon_coupling, phonon_shift, active_blocks
):
    vmem = pl.BlockSpec(memory_space=pltpu.VMEM)
    smem = pl.BlockSpec(memory_space=pltpu.SMEM)
    dma = pltpu.SemaphoreType.DMA
    sigma_l, sigma_g, current, ldos = pl.pallas_call(
        kernel,
        out_shape=(
            jax.ShapeDtypeStruct((NE, 2, 8, NO), BF16),
            jax.ShapeDtypeStruct((NE, 2, 8, NO), BF16),
            jax.ShapeDtypeStruct((1, NB), F32),
            jax.ShapeDtypeStruct((1, NB), F32),
        ),
        in_specs=[vmem] * 5 + [smem] * 2,
        out_specs=[vmem] * 4,
        scratch_shapes=[
            pltpu.VMEM((NB + 1, 2 * NO, NO), BF16),
            pltpu.VMEM((NB, NO, NO), BF16),
            pltpu.VMEM((2 * NO, NO), BF16),
            pltpu.VMEM((2 * NO, NO), BF16),
            pltpu.VMEM((2, NE * 16, NO), F32),
            pltpu.VMEM((2, NE, 16, NO), BF16),
            pltpu.VMEM((NE + 2 * PAD, 16, NO), BF16),
            pltpu.VMEM((NE + 2 * PAD, 16, NO), BF16),
            pltpu.VMEM((16, NO), F32),
            pltpu.VMEM((2, SIDE, 8, NO), F32),
            dma((2,)), dma((2,)), dma((2,)), dma((2,)), dma((2,)), dma((2,)),
        ],
        compiler_params=pltpu.CompilerParams(
            collective_id=0, has_side_effects=True, vmem_limit_bytes=32 << 20
        ),
        name="born_step",
    )(
        green_ret.reshape(NB, NO, NO),
        prior_less.reshape(NB, NO, NO),
        prior_great.reshape(NB, NO, NO),
        coupling,
        phonon_coupling,
        phonon_shift,
        active_blocks,
    )
    shape = (NE, NB, 2, NO)
    return sigma_l.reshape(shape), sigma_g.reshape(shape), current, ldos


def solution(mesh):
    return jax.shard_map(
        local,
        mesh=mesh,
        in_specs=(
            P("energy", "space", None, None),
            P("energy", "space", None, None),
            P("energy", "space", None, None),
            P("space", None, None),
            P("energy", None),
            P(),
            P(),
        ),
        out_specs=(
            P(None, "space", "energy", None),
            P(None, "space", "energy", None),
            P("energy", "space"),
            P("energy", "space"),
        ),
        check_vma=False,
    )
```

```python
import functools

import jax
import jax.numpy as jnp
from jax import lax
from jax.experimental import pallas as pl
from jax.experimental.pallas import tpu as pltpu
from jax.sharding import PartitionSpec as P

phonon_occupation = 0.5
MESH = pl.DeviceIdType.MESH
F32 = jnp.float32
BF16 = jnp.bfloat16

NE = 64
NB = 8
NO = 128
HALF = 4
PAD = 32
SIDE = 8


def dot(left, right):
    return jnp.dot(left, right, preferred_element_type=F32)


def dot_t(left, right):
    return lax.dot_general(left, right, (((1,), (1,)), ((), ())), preferred_element_type=F32)


def side_by_side(stacked):
    return jnp.concatenate([stacked[:NO], stacked[NO:]], axis=1)


def stacked(wide):
    return jnp.concatenate([wide[:, :NO], wide[:, NO:]], axis=0)


def kernel(
    g_hbm, pl_hbm, pg_hbm, c_hbm, pc_hbm, shift_hbm, active_hbm,
    sl_ref, sg_ref, cur_ref, ldos_ref,
    g_ref, pl_ref, pg_ref, c_ref, pc_ref, shift_ref, active_ref, in_sem,
    bare, ct, up_out, up_in, rows, send, recv_low, recv_high, part, total,
    halo_send, halo_recv, x_send, x_recv, t_send, t_recv,
):
    me = lax.axis_index("energy")
    space = lax.axis_index("space")
    spaces = lax.axis_size("space")
    recvs = (recv_low, recv_high)

    fetches = [
        pltpu.make_async_copy(source, target, in_sem.at[i])
        for i, (source, target) in enumerate((
            (g_hbm, g_ref), (pl_hbm, pl_ref), (pg_hbm, pg_ref), (c_hbm, c_ref),
            (pc_hbm, pc_ref), (shift_hbm, shift_ref), (active_hbm, active_ref),
        ))
    ]
    for fetch in fetches:
        fetch.start()

    z, y = me // SIDE, me % SIDE
    in_y = [lax.rem(y + k, SIDE) for k in range(SIDE)]
    in_z = [lax.rem(z + k, SIDE) * SIDE for k in range(SIDE)]
    steps = (1, 7, 2, 6, 3, 5, 4, 0)
    peers = [in_z[(dy + j) % SIDE] + in_y[dy] for j in (4, 0, 2, 6, 1, 5, 3, 7) for dy in steps if j or dy]

    barrier = pltpu.get_barrier_semaphore()

    for p in peers:
        pl.semaphore_signal(barrier, inc=1, device_id={"energy": p}, device_id_type=MESH)

    @pl.when(space > 0)
    def _():
        pl.semaphore_signal(barrier, inc=1, device_id={"space": space - 1}, device_id_type=MESH)

    @pl.when(space < spaces - 1)
    def _():
        pl.semaphore_signal(barrier, inc=1, device_id={"space": space + 1}, device_id_type=MESH)

    row_id = lax.broadcasted_iota(jnp.int32, (NO, NO), 0)
    col_id = lax.broadcasted_iota(jnp.int32, (NO, NO), 1)
    original = 2 * (row_id % NE) + row_id // NE
    select = col_id == original
    permute = jnp.where(select, F32(1), F32(0)).astype(BF16)
    diagonal = jnp.where(select, F32(1), F32(0))

    def prior(b):
        return jnp.concatenate([pl_ref[b], pg_ref[b]], axis=0)

    def make_bare(b):
        wide = jnp.concatenate([pl_ref[b], pg_ref[b]], axis=1)
        half = dot(g_ref[b], wide).astype(BF16)
        bare[b] = dot_t(stacked(half), g_ref[b]).astype(BF16)

    def rise(b):
        return stacked(dot(ct[b], side_by_side(bare[b])).astype(BF16))

    for g in range(2):
        recvs[g][0:PAD] = jnp.zeros((PAD, 16, NO), BF16)
        recvs[g][PAD + NE :] = jnp.zeros((PAD, 16, NO), BF16)
    for fetch in fetches:
        fetch.wait()
    for b in range(NB):
        ct[b] = c_ref[b].T

    make_bare(0)
    make_bare(NB - 1)
    up_out[...] = dot(rise(NB - 1), c_ref[NB - 1]).astype(BF16)

    neighbours = (space > 0).astype(jnp.int32) + (space < spaces - 1).astype(jnp.int32)
    pl.semaphore_wait(barrier, NE - 1 + neighbours)

    down_copy = pltpu.make_async_remote_copy(
        src_ref=bare.at[0], dst_ref=bare.at[NB], send_sem=halo_send.at[0], recv_sem=halo_recv.at[0],
        device_id={"space": lax.rem(space + spaces - 1, spaces)}, device_id_type=MESH,
    )
    up_copy = pltpu.make_async_remote_copy(
        src_ref=up_out, dst_ref=up_in, send_sem=halo_send.at[1], recv_sem=halo_recv.at[1],
        device_id={"space": lax.rem(space + 1, spaces)}, device_id_type=MESH,
    )

    @pl.when(space > 0)
    def _():
        down_copy.start()

    @pl.when(space < spaces - 1)
    def _():
        up_copy.start()

    for b in range(1, NB - 1):
        make_bare(b)

    @pl.when(space == 0)
    def _():
        up_in[...] = jnp.zeros_like(up_in)

    @pl.when(space == spaces - 1)
    def _():
        bare[NB] = jnp.zeros((2 * NO, NO), BF16)

    open_count = active_ref[me]
    lane8 = lax.broadcasted_iota(jnp.int32, (8, NO), 1)
    sub8 = lax.broadcasted_iota(jnp.int32, (8, NO), 0)

    def finish(b, ldos):
        fall = stacked(dot(c_ref[b], side_by_side(bare[b + 1])).astype(BF16))
        if b == 0:
            hops = dot(fall, ct[0]) + up_in[...].astype(F32)
        else:
            left = jnp.concatenate([rise(b - 1), fall], axis=1)
            right = jnp.concatenate([c_ref[b - 1], ct[b]], axis=0)
            hops = dot(left, right)
        source = (prior(b).astype(F32) + hops).astype(BF16)
        mine = dot(permute, g_ref[b]).astype(BF16)
        half = dot(mine, side_by_side(source)).astype(BF16)
        result = dot_t(stacked(half), g_ref[b])
        result = result * jnp.where(space * NB + b < open_count, F32(1), F32(0))
        trace = jnp.sum((result[:NO] + result[NO:]) * diagonal, axis=0, keepdims=True)
        g, inside = b // HALF, b % HALF
        for kind in range(2):
            for r in range(2):
                start = kind * 8 + inside * 2 + r
                at = kind * NO + r * NE
                rows[g, pl.ds(start, NE, stride=16), :] = result[at : at + NE]
        return jnp.where(sub8 == b, jnp.broadcast_to(trace, (8, NO)), ldos)

    def exchange(g, p):
        return pltpu.make_async_remote_copy(
            src_ref=send.at[g, p], dst_ref=recvs[g].at[PAD + me], send_sem=x_send.at[g], recv_sem=x_recv.at[g],
            device_id={"energy": p}, device_id_type=MESH,
        )

    def send_half(g):
        send[g] = rows[g].reshape(NE, 16, NO).astype(BF16)
        for p in peers:
            exchange(g, p).start()
        recvs[g][PAD + me] = send[g, me]

    def whole(g):
        return pltpu.make_async_remote_copy(
            src_ref=send.at[g, pl.ds(0, NE - 1)], dst_ref=recvs[g].at[pl.ds(0, NE - 1)],
            send_sem=x_send.at[g], recv_sem=x_recv.at[g],
            device_id={"energy": (me + 1) % NE}, device_id_type=MESH,
        )

    ldos = jnp.zeros((8, NO), F32)

    @pl.when(space < spaces - 1)
    def _():
        down_copy.wait_recv()

    for b in range(HALF, NB):
        ldos = finish(b, ldos)
    send_half(1)

    @pl.when(space > 0)
    def _():
        up_copy.wait_recv()

    for b in range(HALF):
        ldos = finish(b, ldos)
    send_half(0)

    def as_row(columns):
        sums = jnp.sum(columns, axis=1, keepdims=True)
        return jnp.sum(jnp.where(lane8 == sub8, sums, F32(0)), axis=0, keepdims=True)[:, :NB]

    ldos_ref[...] = as_row(ldos) / NO

    occupied = F32(phonon_occupation)
    coupling8 = jnp.where(sub8 % 2 == 0, pc_ref[0:1, :], pc_ref[1:2, :])
    strong, weak = coupling8 * (1 + occupied), coupling8 * occupied
    s0, s1 = shift_ref[0], shift_ref[1]

    def sigma(g):
        whole(g).wait_recv()
        recv = recvs[g]

        def step(e, acc):
            at = PAD + e
            here = recv[at].astype(F32)
            up = recv[at + s0].astype(F32) + recv[at + s1].astype(F32)
            down = recv[at - s0].astype(F32) + recv[at - s1].astype(F32)
            less = (strong * up[:8] + weak * down[:8]).astype(BF16)
            great = (strong * down[8:] + weak * up[8:]).astype(BF16)
            sl_ref[e, g] = less
            sg_ref[e, g] = great
            flow = less.astype(F32) * here[8:] - great.astype(F32) * here[:8]
            sums = jnp.sum(flow, axis=1, keepdims=True)
            return jnp.where(lane8 == e, sums, acc)

        part[pl.ds(8 * g, 8), :] = lax.fori_loop(0, NE, step, jnp.zeros((8, NO), F32), unroll=8)

    sigma(1)
    sigma(0)

    value = part[pl.ds(0, 8, stride=2), :] + part[pl.ds(1, 8, stride=2), :]
    for phase in range(2):
        mine = y if phase == 0 else z
        total[phase, mine] = value

        def hop(k, phase=phase, mine=mine):
            there = (mine + k) % SIDE
            peer = z * SIDE + there if phase == 0 else there * SIDE + y
            return pltpu.make_async_remote_copy(
                src_ref=total.at[phase, mine], dst_ref=total.at[phase, mine],
                send_sem=t_send.at[phase], recv_sem=t_recv.at[phase],
                device_id={"energy": peer}, device_id_type=MESH,
            )

        for k in range(1, SIDE):
            hop(k).start()
        everything = pltpu.make_async_remote_copy(
            src_ref=total.at[phase, pl.ds(0, SIDE - 1)], dst_ref=total.at[phase, pl.ds(0, SIDE - 1)],
            send_sem=t_send.at[phase], recv_sem=t_recv.at[phase],
            device_id={"energy": (me + 1) % NE}, device_id_type=MESH,
        )
        everything.wait_recv()
        value = jnp.sum(total[phase], axis=0)
        everything.wait_send()

    cur_ref[...] = as_row(jnp.where(lane8 == me, value, F32(0))) / NO

    @pl.when(space > 0)
    def _():
        down_copy.wait_send()

    @pl.when(space < spaces - 1)
    def _():
        up_copy.wait_send()

    whole(1).wait_send()
    whole(0).wait_send()


def keep(*refs):
    copies = [pltpu.make_async_copy(refs[i], refs[4 + i], refs[8].at[i]) for i in range(4)]
    for copy in copies:
        copy.start()
    for copy in copies:
        copy.wait()


def local(
    green_ret, prior_less, prior_great, coupling, phonon_coupling, phonon_shift, active_blocks
):
    vmem = pl.BlockSpec(memory_space=pltpu.VMEM)
    hbm = pl.BlockSpec(memory_space=pltpu.HBM)
    dma = pltpu.SemaphoreType.DMA
    sigma_l, sigma_g, current, ldos = pl.pallas_call(
        kernel,
        out_shape=(
            jax.ShapeDtypeStruct((NE, 2, 8, NO), BF16),
            jax.ShapeDtypeStruct((NE, 2, 8, NO), BF16),
            jax.ShapeDtypeStruct((1, NB), F32),
            jax.ShapeDtypeStruct((1, NB), F32),
        ),
        in_specs=[hbm] * 7,
        out_specs=[vmem] * 4,
        scratch_shapes=[
            pltpu.VMEM((NB, NO, NO), BF16),
            pltpu.VMEM((NB, NO, NO), BF16),
            pltpu.VMEM((NB, NO, NO), BF16),
            pltpu.VMEM((NB, NO, NO), BF16),
            pltpu.VMEM((2, NO), F32),
            pltpu.SMEM((2,), jnp.int32),
            pltpu.SMEM((NE,), jnp.int32),
            dma((7,)),
            pltpu.VMEM((NB + 1, 2 * NO, NO), BF16),
            pltpu.VMEM((NB, NO, NO), BF16),
            pltpu.VMEM((2 * NO, NO), BF16),
            pltpu.VMEM((2 * NO, NO), BF16),
            pltpu.VMEM((2, NE * 16, NO), F32),
            pltpu.VMEM((2, NE, 16, NO), BF16),
            pltpu.VMEM((NE + 2 * PAD, 16, NO), BF16),
            pltpu.VMEM((NE + 2 * PAD, 16, NO), BF16),
            pltpu.VMEM((16, NO), F32),
            pltpu.VMEM((2, SIDE, 8, NO), F32),
            dma((2,)), dma((2,)), dma((2,)), dma((2,)), dma((2,)), dma((2,)),
        ],
        compiler_params=pltpu.CompilerParams(
            collective_id=0, has_side_effects=True, vmem_limit_bytes=60 << 20
        ),
        name="born_step",
    )(
        green_ret.reshape(NB, NO, NO),
        prior_less.reshape(NB, NO, NO),
        prior_great.reshape(NB, NO, NO),
        coupling,
        phonon_coupling,
        phonon_shift,
        active_blocks,
    )
    results = (sigma_l, sigma_g, current, ldos)
    sigma_l, sigma_g, current, ldos = pl.pallas_call(
        keep,
        out_shape=tuple(jax.ShapeDtypeStruct(r.shape, r.dtype) for r in results),
        in_specs=[vmem] * 4,
        out_specs=[hbm] * 4,
        scratch_shapes=[dma((4,))],
        name="keep",
    )(*results)
    shape = (NE, NB, 2, NO)
    return sigma_l.reshape(shape), sigma_g.reshape(shape), current, ldos


def solution(mesh):
    return jax.shard_map(
        local,
        mesh=mesh,
        in_specs=(
            P("energy", "space", None, None),
            P("energy", "space", None, None),
            P("energy", "space", None, None),
            P("space", None, None),
            P("energy", None),
            P(),
            P(),
        ),
        out_specs=(
            P(None, "space", "energy", None),
            P(None, "space", "energy", None),
            P("energy", "space"),
            P("energy", "space"),
        ),
        check_vma=False,
    )
```

```python
import functools

import jax
import jax.numpy as jnp
from jax import lax
from jax.experimental import pallas as pl
from jax.experimental.pallas import tpu as pltpu
from jax.sharding import PartitionSpec as P

phonon_occupation = 0.5
MESH = pl.DeviceIdType.MESH
F32 = jnp.float32
BF16 = jnp.bfloat16

NE = 64
NB = 8
NO = 128
HALF = 4
PAD = 32
SIDE = 8


def dot(left, right):
    return jnp.dot(left, right, preferred_element_type=F32)


def dot_t(left, right):
    return lax.dot_general(left, right, (((1,), (1,)), ((), ())), preferred_element_type=F32)


def side_by_side(stacked):
    return jnp.concatenate([stacked[:NO], stacked[NO:]], axis=1)


def stacked(wide):
    return jnp.concatenate([wide[:, :NO], wide[:, NO:]], axis=0)


def kernel(
    g_hbm, pl_hbm, pg_hbm, c_hbm, pc_hbm, shift_hbm, active_hbm,
    sl_ref, sg_ref, cur_ref, ldos_ref,
    g_ref, pl_ref, pg_ref, c_ref, pc_ref, shift_ref, active_ref, in_sem,
    bare, ct, up_out, up_in, rows, send, recv_low, recv_high, early, part, flows, total,
    halo_send, halo_recv, x_send, x_recv, t_send, t_recv,
):
    me = lax.axis_index("energy")
    space = lax.axis_index("space")
    spaces = lax.axis_size("space")
    recvs = (recv_low, recv_high)

    fetches = [
        pltpu.make_async_copy(source, target, in_sem.at[i])
        for i, (source, target) in enumerate((
            (g_hbm, g_ref), (pl_hbm, pl_ref), (pg_hbm, pg_ref), (c_hbm, c_ref),
            (pc_hbm, pc_ref), (shift_hbm, shift_ref), (active_hbm, active_ref),
        ))
    ]
    for fetch in fetches:
        fetch.start()

    z, y = me // SIDE, me % SIDE
    in_y = [lax.rem(y + k, SIDE) for k in range(SIDE)]
    in_z = [lax.rem(z + k, SIDE) * SIDE for k in range(SIDE)]
    steps = (1, 7, 2, 6, 3, 5, 4, 0)
    offsets = [(dy, (dy + j) % SIDE) for j in (4, 0, 2, 6, 1, 5, 3, 7) for dy in steps if j or dy]
    offsets.sort(key=lambda at: -sum(min(d, SIDE - d) for d in at))
    peers = [in_z[dz] + in_y[dy] for dy, dz in offsets]

    barrier = pltpu.get_barrier_semaphore()

    for p in peers:
        pl.semaphore_signal(barrier, inc=1, device_id={"energy": p}, device_id_type=MESH)

    @pl.when(space > 0)
    def _():
        pl.semaphore_signal(barrier, inc=1, device_id={"space": space - 1}, device_id_type=MESH)

    @pl.when(space < spaces - 1)
    def _():
        pl.semaphore_signal(barrier, inc=1, device_id={"space": space + 1}, device_id_type=MESH)

    row_id = lax.broadcasted_iota(jnp.int32, (NO, NO), 0)
    col_id = lax.broadcasted_iota(jnp.int32, (NO, NO), 1)
    original = 2 * (row_id % NE) + row_id // NE
    select = col_id == original
    permute = jnp.where(select, F32(1), F32(0)).astype(BF16)
    diagonal = jnp.where(select, F32(1), F32(0))

    def prior(b):
        return jnp.concatenate([pl_ref[b], pg_ref[b]], axis=0)

    def make_bare(b):
        wide = jnp.concatenate([pl_ref[b], pg_ref[b]], axis=1)
        half = dot(g_ref[b], wide).astype(BF16)
        bare[b] = dot_t(stacked(half), g_ref[b]).astype(BF16)

    def rise(b):
        return stacked(dot(ct[b], side_by_side(bare[b])).astype(BF16))

    for g in range(2):
        recvs[g][0:PAD] = jnp.zeros((PAD, 16, NO), BF16)
        recvs[g][PAD + NE :] = jnp.zeros((PAD, 16, NO), BF16)
    for fetch in fetches:
        fetch.wait()
    for b in range(NB):
        ct[b] = c_ref[b].T

    make_bare(0)
    make_bare(NB - 1)
    up_out[...] = dot(rise(NB - 1), c_ref[NB - 1]).astype(BF16)

    open_count = active_ref[me]
    lane8 = lax.broadcasted_iota(jnp.int32, (8, NO), 1)
    sub8 = lax.broadcasted_iota(jnp.int32, (8, NO), 0)

    def finish(b, ldos):
        fall = stacked(dot(c_ref[b], side_by_side(bare[b + 1])).astype(BF16))
        if b == 0:
            hops = dot(fall, ct[0]) + up_in[...].astype(F32)
        else:
            left = jnp.concatenate([rise(b - 1), fall], axis=1)
            right = jnp.concatenate([c_ref[b - 1], ct[b]], axis=0)
            hops = dot(left, right)
        source = (prior(b).astype(F32) + hops).astype(BF16)
        mine = dot(permute, g_ref[b]).astype(BF16)
        half = dot(mine, side_by_side(source)).astype(BF16)
        result = dot_t(stacked(half), g_ref[b])
        result = result * jnp.where(space * NB + b < open_count, F32(1), F32(0))
        trace = jnp.sum((result[:NO] + result[NO:]) * diagonal, axis=0, keepdims=True)
        g, inside = int(b in (1, 2, 3, 4)), b % HALF
        for kind in range(2):
            for r in range(2):
                start = kind * 8 + inside * 2 + r
                at = kind * NO + r * NE
                rows[g, pl.ds(start, NE, stride=16), :] = result[at : at + NE]
        return jnp.where(sub8 == b, jnp.broadcast_to(trace, (8, NO)), ldos)

    def exchange(g, p):
        return pltpu.make_async_remote_copy(
            src_ref=send.at[g, p], dst_ref=recvs[g].at[PAD + me], send_sem=x_send.at[g], recv_sem=x_recv.at[g],
            device_id={"energy": p}, device_id_type=MESH,
        )

    def pack(g):
        send[g] = rows[g].reshape(NE, 16, NO).astype(BF16)

    def start(g, targets):
        for p in targets:
            exchange(g, p).start()

    def whole(g):
        return pltpu.make_async_remote_copy(
            src_ref=send.at[g, pl.ds(0, NE - 1)], dst_ref=recvs[g].at[pl.ds(0, NE - 1)],
            send_sem=x_send.at[g], recv_sem=x_recv.at[g],
            device_id={"energy": (me + 1) % NE}, device_id_type=MESH,
        )

    ldos = jnp.zeros((8, NO), F32)
    for b in range(1, NB - 1):
        make_bare(b)
    @pl.when(space == 0)
    def _():
        up_in[...] = jnp.zeros_like(up_in)

    @pl.when(space == spaces - 1)
    def _():
        bare[NB] = jnp.zeros((2 * NO, NO), BF16)

    for b in (1, 2, 3, 4):
        ldos = finish(b, ldos)
    pack(1)

    neighbours = (space > 0).astype(jnp.int32) + (space < spaces - 1).astype(jnp.int32)
    pl.semaphore_wait(barrier, NE - 1 + neighbours)

    down_copy = pltpu.make_async_remote_copy(
        src_ref=bare.at[0], dst_ref=bare.at[NB], send_sem=halo_send.at[0], recv_sem=halo_recv.at[0],
        device_id={"space": lax.rem(space + spaces - 1, spaces)}, device_id_type=MESH,
    )
    up_copy = pltpu.make_async_remote_copy(
        src_ref=up_out, dst_ref=up_in, send_sem=halo_send.at[1], recv_sem=halo_recv.at[1],
        device_id={"space": lax.rem(space + 1, spaces)}, device_id_type=MESH,
    )

    @pl.when(space > 0)
    def _():
        down_copy.start()

    @pl.when(space < spaces - 1)
    def _():
        up_copy.start()

    start(1, peers[:24])
    ldos = finish(5, ldos)
    start(1, peers[24:48])
    ldos = finish(6, ldos)
    start(1, peers[48:])

    @pl.when(space < spaces - 1)
    def _():
        down_copy.wait_recv()

    ldos = finish(7, ldos)

    @pl.when(space > 0)
    def _():
        up_copy.wait_recv()

    ldos = finish(0, ldos)
    pack(0)
    start(0, peers)
    for g in range(2):
        recvs[g][PAD + me] = send[g, me]

    def as_row(columns):
        sums = jnp.sum(columns, axis=1, keepdims=True)
        return jnp.sum(jnp.where(lane8 == sub8, sums, F32(0)), axis=0, keepdims=True)[:, :NB]

    ldos_ref[...] = as_row(ldos) / NO

    occupied = F32(phonon_occupation)
    coupling8 = jnp.where(sub8 % 2 == 0, pc_ref[0:1, :], pc_ref[1:2, :])
    strong, weak = coupling8 * (1 + occupied), coupling8 * occupied
    s0, s1 = shift_ref[0], shift_ref[1]

    first = sub8 < 2
    place1 = jnp.where(first, sub8 + 8, sub8)
    place0 = jnp.where(first, sub8, sub8 + 8)

    def sigma(g):
        whole(g).wait_recv()
        recv = recvs[g]

        def step(e, carry):
            at = PAD + e
            here = recv[at].astype(F32)
            up = recv[at + s0].astype(F32) + recv[at + s1].astype(F32)
            down = recv[at - s0].astype(F32) + recv[at - s1].astype(F32)
            less = (strong * up[:8] + weak * down[:8]).astype(BF16).astype(F32)
            great = (strong * down[8:] + weak * up[8:]).astype(BF16).astype(F32)
            if g == 1:
                early[0, e] = less
                early[1, e] = great
            else:
                for out, before, now in ((sl_ref, early[0, e], less), (sg_ref, early[1, e], great)):
                    low = jnp.where(first, now, before)
                    high = jnp.where(first, before, now)
                    out[e] = jnp.concatenate([low, high], axis=0).astype(BF16)
            flow = less * here[8:] - great * here[:8]
            sums = jnp.where(lane8 == (place1 if g == 1 else place0), jnp.sum(flow, axis=1, keepdims=True), F32(0))
            if g == 1:
                part[e] = sums
            else:
                flows[e] = jnp.sum(part[e] + sums, axis=0, keepdims=True)
            return carry

        lax.fori_loop(0, NE, step, 0, unroll=8)

    sigma(1)
    sigma(0)

    def share(p):
        return pltpu.make_async_remote_copy(
            src_ref=flows.at[p], dst_ref=total.at[me], send_sem=t_send, recv_sem=t_recv,
            device_id={"energy": p}, device_id_type=MESH,
        )

    for p in peers:
        share(p).start()
    total[me] = flows[me]
    shares = pltpu.make_async_remote_copy(
        src_ref=flows.at[pl.ds(0, NE - 1)], dst_ref=total.at[pl.ds(0, NE - 1)], send_sem=t_send, recv_sem=t_recv,
        device_id={"energy": peers[0]}, device_id_type=MESH,
    )
    shares.wait_recv()
    lanes = [total[e] for e in range(NE)]
    while len(lanes) > 1:
        lanes = [one + other for one, other in zip(lanes[::2], lanes[1::2])]
    cur_ref[...] = as_row(jnp.where(lane8 // 2 == sub8, jnp.broadcast_to(lanes[0], (8, NO)), F32(0))) / NO
    shares.wait_send()

    @pl.when(space > 0)
    def _():
        down_copy.wait_send()

    @pl.when(space < spaces - 1)
    def _():
        up_copy.wait_send()

    whole(1).wait_send()
    whole(0).wait_send()


def keep(*refs):
    copies = [pltpu.make_async_copy(refs[i], refs[4 + i], refs[8].at[i]) for i in range(4)]
    for copy in copies:
        copy.start()
    for copy in copies:
        copy.wait()


def local(
    green_ret, prior_less, prior_great, coupling, phonon_coupling, phonon_shift, active_blocks
):
    vmem = pl.BlockSpec(memory_space=pltpu.VMEM)
    hbm = pl.BlockSpec(memory_space=pltpu.HBM)
    dma = pltpu.SemaphoreType.DMA
    sigma_l, sigma_g, current, ldos = pl.pallas_call(
        kernel,
        out_shape=(
            jax.ShapeDtypeStruct((NE, 2 * NB, NO), BF16),
            jax.ShapeDtypeStruct((NE, 2 * NB, NO), BF16),
            jax.ShapeDtypeStruct((1, NB), F32),
            jax.ShapeDtypeStruct((1, NB), F32),
        ),
        in_specs=[hbm] * 7,
        out_specs=[vmem] * 4,
        scratch_shapes=[
            pltpu.VMEM((NB, NO, NO), BF16),
            pltpu.VMEM((NB, NO, NO), BF16),
            pltpu.VMEM((NB, NO, NO), BF16),
            pltpu.VMEM((NB, NO, NO), BF16),
            pltpu.VMEM((2, NO), F32),
            pltpu.SMEM((2,), jnp.int32),
            pltpu.SMEM((NE,), jnp.int32),
            dma((7,)),
            pltpu.VMEM((NB + 1, 2 * NO, NO), BF16),
            pltpu.VMEM((NB, NO, NO), BF16),
            pltpu.VMEM((2 * NO, NO), BF16),
            pltpu.VMEM((2 * NO, NO), BF16),
            pltpu.VMEM((2, NE * 16, NO), F32),
            pltpu.VMEM((2, NE, 16, NO), BF16),
            pltpu.VMEM((NE + 2 * PAD, 16, NO), BF16),
            pltpu.VMEM((NE + 2 * PAD, 16, NO), BF16),
            pltpu.VMEM((2, NE, 8, NO), F32),
            pltpu.VMEM((NE, 8, NO), F32),
            pltpu.VMEM((NE, 1, NO), F32),
            pltpu.VMEM((NE, 1, NO), F32),
            dma((2,)), dma((2,)), dma((2,)), dma((2,)), dma, dma,
        ],
        compiler_params=pltpu.CompilerParams(
            collective_id=0, has_side_effects=True, vmem_limit_bytes=60 << 20
        ),
        name="born_step",
    )(
        green_ret.reshape(NB, NO, NO),
        prior_less.reshape(NB, NO, NO),
        prior_great.reshape(NB, NO, NO),
        coupling,
        phonon_coupling,
        phonon_shift,
        active_blocks,
    )
    results = (sigma_l, sigma_g, current, ldos)
    sigma_l, sigma_g, current, ldos = pl.pallas_call(
        keep,
        out_shape=tuple(jax.ShapeDtypeStruct(r.shape, r.dtype) for r in results),
        in_specs=[vmem] * 4,
        out_specs=[hbm] * 4,
        scratch_shapes=[dma((4,))],
        name="keep",
    )(*results)
    shape = (NE, NB, 2, NO)
    return sigma_l.reshape(shape), sigma_g.reshape(shape), current, ldos


def solution(mesh):
    return jax.shard_map(
        local,
        mesh=mesh,
        in_specs=(
            P("energy", "space", None, None),
            P("energy", "space", None, None),
            P("energy", "space", None, None),
            P("space", None, None),
            P("energy", None),
            P(),
            P(),
        ),
        out_specs=(
            P(None, "space", "energy", None),
            P(None, "space", "energy", None),
            P("energy", "space"),
            P("energy", "space"),
        ),
        check_vma=False,
    )
```

```python
import functools

import jax
import jax.numpy as jnp
from jax import lax
from jax.experimental import pallas as pl
from jax.experimental.pallas import tpu as pltpu
from jax.sharding import PartitionSpec as P

phonon_occupation = 0.5
MESH = pl.DeviceIdType.MESH
F32 = jnp.float32
BF16 = jnp.bfloat16

NE = 64
NB = 8
NO = 128
HALF = 4
PAD = 32
CUTS = 2
SIDE = 8


def dot(left, right):
    return jnp.dot(left, right, preferred_element_type=F32)


def dot_t(left, right):
    return lax.dot_general(left, right, (((1,), (1,)), ((), ())), preferred_element_type=F32)


def side_by_side(stacked):
    return jnp.concatenate([stacked[:NO], stacked[NO:]], axis=1)


def stacked(wide):
    return jnp.concatenate([wide[:, :NO], wide[:, NO:]], axis=0)


def kernel(
    g_hbm, pl_hbm, pg_hbm, c_hbm, pc_hbm, shift_hbm, active_hbm,
    sl_ref, sg_ref, cur_ref, ldos_ref,
    g_ref, pl_ref, pg_ref, c_ref, pc_ref, shift_ref, active_ref, in_sem,
    left, source, half, mixed, bare, ct, up_out, up_in, rows, send, recv_low, recv_high, early, part, flows, total,
    halo_send, halo_recv, x_send, x_recv, t_send, t_recv,
):
    me = lax.axis_index("energy")
    space = lax.axis_index("space")
    spaces = lax.axis_size("space")
    recvs = (recv_low, recv_high)

    fetches = [
        pltpu.make_async_copy(source, target, in_sem.at[i])
        for i, (source, target) in enumerate((
            (g_hbm, g_ref), (pl_hbm, pl_ref), (pg_hbm, pg_ref), (c_hbm, c_ref),
            (pc_hbm, pc_ref), (shift_hbm, shift_ref), (active_hbm, active_ref),
        ))
    ]
    for fetch in fetches[:4]:
        fetch.start()

    z, y = me // SIDE, me % SIDE
    in_y = [lax.rem(y + k, SIDE) for k in range(SIDE)]
    in_z = [lax.rem(z + k, SIDE) * SIDE for k in range(SIDE)]
    steps = (1, 7, 2, 6, 3, 5, 4, 0)
    offsets = [(dy, (dy + j) % SIDE) for j in (4, 0, 2, 6, 1, 5, 3, 7) for dy in steps if j or dy]
    offsets.sort(key=lambda at: -sum(min(d, SIDE - d) for d in at))
    peers = [in_z[dz] + in_y[dy] for dy, dz in offsets]

    barrier = pltpu.get_barrier_semaphore()

    for p in peers:
        pl.semaphore_signal(barrier, inc=1, device_id={"energy": p}, device_id_type=MESH)

    @pl.when(space > 0)
    def _():
        pl.semaphore_signal(barrier, inc=1, device_id={"space": space - 1}, device_id_type=MESH)

    @pl.when(space < spaces - 1)
    def _():
        pl.semaphore_signal(barrier, inc=1, device_id={"space": space + 1}, device_id_type=MESH)

    for fetch in fetches[4:]:
        fetch.start()

    row_id = lax.broadcasted_iota(jnp.int32, (NO, NO), 0)
    col_id = lax.broadcasted_iota(jnp.int32, (NO, NO), 1)
    original = 2 * (row_id % NE) + row_id // NE
    select = col_id == original
    permute = jnp.where(select, F32(1), F32(0)).astype(BF16)
    diagonal = jnp.where(select, F32(1), F32(0))

    def prior(b):
        return jnp.concatenate([pl_ref[b], pg_ref[b]], axis=0)

    def make_bare(b):
        wide = jnp.concatenate([pl_ref[b], pg_ref[b]], axis=1)
        half = dot(g_ref[b], wide).astype(BF16)
        bare[b] = dot_t(stacked(half), g_ref[b]).astype(BF16)

    def rise(b):
        return stacked(dot(ct[b], side_by_side(bare[b])).astype(BF16))

    for g in range(2):
        recvs[g][0:PAD] = jnp.zeros((PAD, 16, NO), BF16)
        recvs[g][PAD + NE :] = jnp.zeros((PAD, 16, NO), BF16)
    for fetch in fetches:
        fetch.wait()
    for b in range(NB):
        ct[b] = c_ref[b].T
        mixed[b] = dot(permute, g_ref[b]).astype(BF16)

    make_bare(0)
    make_bare(NB - 1)
    up_out[...] = dot(rise(NB - 1), c_ref[NB - 1]).astype(BF16)

    open_count = active_ref[me]
    lane8 = lax.broadcasted_iota(jnp.int32, (8, NO), 1)
    sub8 = lax.broadcasted_iota(jnp.int32, (8, NO), 0)

    def finish(blocks, ldos):
        for b in blocks:
            fall = stacked(dot(c_ref[b], side_by_side(bare[b + 1])).astype(BF16))
            if b == 0:
                left[0, :, :NO] = fall
            else:
                left[b] = jnp.concatenate([rise(b - 1), fall], axis=1)
        for b in blocks:
            if b == 0:
                hops = dot(left[0, :, :NO], ct[0]) + up_in[...].astype(F32)
            else:
                hops = dot(left[b], jnp.concatenate([c_ref[b - 1], ct[b]], axis=0))
            source[b] = side_by_side((prior(b).astype(F32) + hops).astype(BF16))
        for b in blocks:
            half[b] = stacked(dot(mixed[b], source[b]).astype(BF16))
        for b in blocks:
            result = dot_t(half[b], g_ref[b])
            result = result * jnp.where(space * NB + b < open_count, F32(1), F32(0))
            trace = jnp.sum((result[:NO] + result[NO:]) * diagonal, axis=0, keepdims=True)
            g, inside = int(b in (1, 2, 3, 4)), b % HALF
            for kind in range(2):
                for r in range(2):
                    begin = kind * 8 + inside * 2 + r
                    at = kind * NO + r * NE
                    rows[g, pl.ds(begin, NE, stride=16), :] = result[at : at + NE]
            ldos = jnp.where(sub8 == b, jnp.broadcast_to(trace, (8, NO)), ldos)
        return ldos

    def exchange(g, p):
        return pltpu.make_async_remote_copy(
            src_ref=send.at[g, p], dst_ref=recvs[g].at[PAD + me], send_sem=x_send.at[g], recv_sem=x_recv.at[g],
            device_id={"energy": p}, device_id_type=MESH,
        )

    def pack(g):
        send[g] = rows[g].reshape(NE, 16, NO).astype(BF16)

    def start(g, targets):
        for p in targets:
            exchange(g, p).start()

    def whole(g):
        return pltpu.make_async_remote_copy(
            src_ref=send.at[g, pl.ds(0, NE - 1)], dst_ref=recvs[g].at[pl.ds(0, NE - 1)],
            send_sem=x_send.at[g], recv_sem=x_recv.at[g],
            device_id={"energy": (me + 1) % NE}, device_id_type=MESH,
        )

    ldos = jnp.zeros((8, NO), F32)
    for b in range(1, NB - 1):
        make_bare(b)
    @pl.when(space == 0)
    def _():
        up_in[...] = jnp.zeros_like(up_in)

    @pl.when(space == spaces - 1)
    def _():
        bare[NB] = jnp.zeros((2 * NO, NO), BF16)

    ldos = finish((1, 2, 3, 4), ldos)
    pack(1)

    neighbours = (space > 0).astype(jnp.int32) + (space < spaces - 1).astype(jnp.int32)
    pl.semaphore_wait(barrier, NE - 1 + neighbours)

    down_copy = pltpu.make_async_remote_copy(
        src_ref=bare.at[0], dst_ref=bare.at[NB], send_sem=halo_send.at[0], recv_sem=halo_recv.at[0],
        device_id={"space": lax.rem(space + spaces - 1, spaces)}, device_id_type=MESH,
    )
    up_copy = pltpu.make_async_remote_copy(
        src_ref=up_out, dst_ref=up_in, send_sem=halo_send.at[1], recv_sem=halo_recv.at[1],
        device_id={"space": lax.rem(space + 1, spaces)}, device_id_type=MESH,
    )

    @pl.when(space > 0)
    def _():
        down_copy.start()

    @pl.when(space < spaces - 1)
    def _():
        up_copy.start()

    start(1, peers)

    @pl.when(space < spaces - 1)
    def _():
        down_copy.wait_recv()


    @pl.when(space > 0)
    def _():
        up_copy.wait_recv()

    ldos = finish((5, 6, 7, 0), ldos)
    pack(0)
    start(0, peers)
    for g in range(2):
        recvs[g][PAD + me] = send[g, me]

    def as_row(columns):
        sums = jnp.sum(columns, axis=1, keepdims=True)
        return jnp.sum(jnp.where(lane8 == sub8, sums, F32(0)), axis=0, keepdims=True)[:, :NB]

    ldos_ref[...] = as_row(ldos) / NO

    occupied = F32(phonon_occupation)
    coupling8 = jnp.where(sub8 % 2 == 0, pc_ref[0:1, :], pc_ref[1:2, :])
    strong, weak = coupling8 * (1 + occupied), coupling8 * occupied
    s0, s1 = shift_ref[0], shift_ref[1]

    first = sub8 < 2
    place1 = jnp.where(first, sub8 + 8, sub8)
    place0 = jnp.where(first, sub8, sub8 + 8)

    def sigma(g):
        whole(g).wait_recv()
        recv = recvs[g]

        def step(e, carry):
            at = PAD + e
            here = recv[at].astype(F32)
            up = recv[at + s0].astype(F32) + recv[at + s1].astype(F32)
            down = recv[at - s0].astype(F32) + recv[at - s1].astype(F32)
            less = (strong * up[:8] + weak * down[:8]).astype(BF16).astype(F32)
            great = (strong * down[8:] + weak * up[8:]).astype(BF16).astype(F32)
            early[g, 0, e] = less
            early[g, 1, e] = great
            flow = less * here[8:] - great * here[:8]
            sums = jnp.where(lane8 == (place1 if g == 1 else place0), jnp.sum(flow, axis=1, keepdims=True), F32(0))
            if g == 1:
                part[e] = sums
            else:
                flows[e] = jnp.sum(part[e] + sums, axis=0, keepdims=True)
            return carry

        lax.fori_loop(0, NE, step, 0, unroll=32)

    sigma(1)
    sigma(0)

    def share(p):
        return pltpu.make_async_remote_copy(
            src_ref=flows.at[p], dst_ref=total.at[me], send_sem=t_send, recv_sem=t_recv,
            device_id={"energy": p}, device_id_type=MESH,
        )

    for p in peers:
        share(p).start()
    total[me] = flows[me]

    def merge(e, carry):
        for kind, out in enumerate((sl_ref, sg_ref)):
            low = jnp.where(first, early[0, kind, e], early[1, kind, e])
            high = jnp.where(first, early[1, kind, e], early[0, kind, e])
            out[e] = jnp.concatenate([low, high], axis=0).astype(BF16)
        return carry

    lax.fori_loop(0, NE, merge, 0, unroll=8)
    shares = pltpu.make_async_remote_copy(
        src_ref=flows.at[pl.ds(0, NE - 1)], dst_ref=total.at[pl.ds(0, NE - 1)], send_sem=t_send, recv_sem=t_recv,
        device_id={"energy": peers[0]}, device_id_type=MESH,
    )
    shares.wait_recv()
    lanes = [total[e] for e in range(NE)]
    while len(lanes) > 1:
        lanes = [one + other for one, other in zip(lanes[::2], lanes[1::2])]
    cur_ref[...] = as_row(jnp.where(lane8 // 2 == sub8, jnp.broadcast_to(lanes[0], (8, NO)), F32(0))) / NO
    shares.wait_send()

    @pl.when(space > 0)
    def _():
        down_copy.wait_send()

    @pl.when(space < spaces - 1)
    def _():
        up_copy.wait_send()

    whole(1).wait_send()
    whole(0).wait_send()


def keep(*refs):
    copies = []
    for i in range(2):
        for n in range(CUTS):
            piece = pl.ds(n * (NE // CUTS), NE // CUTS)
            copies.append(pltpu.make_async_copy(refs[i].at[piece], refs[4 + i].at[piece], refs[8].at[4 + CUTS * i + n]))
    copies += [pltpu.make_async_copy(refs[i], refs[4 + i], refs[8].at[i]) for i in (2, 3)]
    for copy in copies:
        copy.start()
    for copy in copies:
        copy.wait()


def local(
    green_ret, prior_less, prior_great, coupling, phonon_coupling, phonon_shift, active_blocks
):
    vmem = pl.BlockSpec(memory_space=pltpu.VMEM)
    hbm = pl.BlockSpec(memory_space=pltpu.HBM)
    dma = pltpu.SemaphoreType.DMA
    sigma_l, sigma_g, current, ldos = pl.pallas_call(
        kernel,
        out_shape=(
            jax.ShapeDtypeStruct((NE, 2 * NB, NO), BF16),
            jax.ShapeDtypeStruct((NE, 2 * NB, NO), BF16),
            jax.ShapeDtypeStruct((1, NB), F32),
            jax.ShapeDtypeStruct((1, NB), F32),
        ),
        in_specs=[hbm] * 7,
        out_specs=[vmem] * 4,
        scratch_shapes=[
            pltpu.VMEM((NB, NO, NO), BF16),
            pltpu.VMEM((NB, NO, NO), BF16),
            pltpu.VMEM((NB, NO, NO), BF16),
            pltpu.VMEM((NB, NO, NO), BF16),
            pltpu.VMEM((2, NO), F32),
            pltpu.SMEM((2,), jnp.int32),
            pltpu.SMEM((NE,), jnp.int32),
            dma((7,)),
            pltpu.VMEM((NB, 2 * NO, 2 * NO), BF16),
            pltpu.VMEM((NB, NO, 2 * NO), BF16),
            pltpu.VMEM((NB, 2 * NO, NO), BF16),
            pltpu.VMEM((NB, NO, NO), BF16),
            pltpu.VMEM((NB + 1, 2 * NO, NO), BF16),
            pltpu.VMEM((NB, NO, NO), BF16),
            pltpu.VMEM((2 * NO, NO), BF16),
            pltpu.VMEM((2 * NO, NO), BF16),
            pltpu.VMEM((2, NE * 16, NO), F32),
            pltpu.VMEM((2, NE, 16, NO), BF16),
            pltpu.VMEM((NE + 2 * PAD, 16, NO), BF16),
            pltpu.VMEM((NE + 2 * PAD, 16, NO), BF16),
            pltpu.VMEM((2, 2, NE, 8, NO), F32),
            pltpu.VMEM((NE, 8, NO), F32),
            pltpu.VMEM((NE, 1, NO), F32),
            pltpu.VMEM((NE, 1, NO), F32),
            dma((2,)), dma((2,)), dma((2,)), dma((2,)), dma, dma,
        ],
        compiler_params=pltpu.CompilerParams(
            collective_id=0, has_side_effects=True, vmem_limit_bytes=32 << 20
        ),
        name="born_step",
    )(
        *(
            pltpu.with_memory_space_constraint(operand, pltpu.HBM)
            for operand in (
                green_ret.reshape(NB, NO, NO),
                prior_less.reshape(NB, NO, NO),
                prior_great.reshape(NB, NO, NO),
                coupling,
                phonon_coupling,
                phonon_shift,
                active_blocks,
            )
        )
    )
    results = (sigma_l, sigma_g, current, ldos)
    sigma_l, sigma_g, current, ldos = pl.pallas_call(
        keep,
        out_shape=tuple(jax.ShapeDtypeStruct(r.shape, r.dtype) for r in results),
        in_specs=[vmem] * 4,
        out_specs=[hbm] * 4,
        scratch_shapes=[dma((4 + 2 * CUTS,))],
        name="keep",
    )(*(pltpu.with_memory_space_constraint(r, pltpu.VMEM) for r in results))
    shape = (NE, NB, 2, NO)
    return sigma_l.reshape(shape), sigma_g.reshape(shape), current, ldos


def solution(mesh):
    return jax.shard_map(
        local,
        mesh=mesh,
        in_specs=(
            P("energy", "space", None, None),
            P("energy", "space", None, None),
            P("energy", "space", None, None),
            P("space", None, None),
            P("energy", None),
            P(),
            P(),
        ),
        out_specs=(
            P(None, "space", "energy", None),
            P(None, "space", "energy", None),
            P("energy", "space"),
            P("energy", "space"),
        ),
        check_vma=False,
    )
```

```python
import functools

import jax
import jax.numpy as jnp
from jax import lax
from jax.experimental import pallas as pl
from jax.experimental.pallas import tpu as pltpu
from jax.sharding import PartitionSpec as P

phonon_occupation = 0.5
MESH = pl.DeviceIdType.MESH
F32 = jnp.float32
BF16 = jnp.bfloat16

NE = 64
NB = 8
NO = 128
HALF = 4
PAD = 32
CUTS = 2
SIDE = 8


def dot(left, right):
    return jnp.dot(left, right, preferred_element_type=F32)


def dot_t(left, right):
    return lax.dot_general(left, right, (((1,), (1,)), ((), ())), preferred_element_type=F32)


def side_by_side(stacked):
    return jnp.concatenate([stacked[:NO], stacked[NO:]], axis=1)


def stacked(wide):
    return jnp.concatenate([wide[:, :NO], wide[:, NO:]], axis=0)


def kernel(
    g_hbm, pl_hbm, pg_hbm, c_hbm, pc_hbm, shift_hbm, active_hbm,
    sl_ref, sg_ref, cur_ref, ldos_ref,
    g_ref, pl_ref, pg_ref, c_ref, pc_ref, shift_ref, active_ref, in_sem,
    left, source, half, mixed, bare, ct, up_out, up_in, rows, send, recv_low, recv_high, early, part, flows, total,
    halo_send, halo_recv, x_send, x_recv, t_send, t_recv,
):
    me = lax.axis_index("energy")
    space = lax.axis_index("space")
    spaces = lax.axis_size("space")
    recvs = (recv_low, recv_high)

    fetches = [
        pltpu.make_async_copy(source, target, in_sem.at[i])
        for i, (source, target) in enumerate((
            (g_hbm, g_ref), (pl_hbm, pl_ref), (pg_hbm, pg_ref), (c_hbm, c_ref),
            (pc_hbm, pc_ref), (shift_hbm, shift_ref), (active_hbm, active_ref),
        ))
    ]

    z, y = me // SIDE, me % SIDE
    in_y = [lax.rem(y + k, SIDE) for k in range(SIDE)]
    in_z = [lax.rem(z + k, SIDE) * SIDE for k in range(SIDE)]
    steps = (1, 7, 2, 6, 3, 5, 4, 0)
    offsets = [(dy, (dy + j) % SIDE) for j in (4, 0, 2, 6, 1, 5, 3, 7) for dy in steps if j or dy]
    offsets.sort(key=lambda at: -sum(min(d, SIDE - d) for d in at))
    peers = [in_z[dz] + in_y[dy] for dy, dz in offsets]

    barrier = pltpu.get_barrier_semaphore()

    for p in peers:
        pl.semaphore_signal(barrier, inc=1, device_id=(p, space), device_id_type=MESH)

    @pl.when(space > 0)
    def _():
        pl.semaphore_signal(barrier, inc=1, device_id={"space": space - 1}, device_id_type=MESH)

    @pl.when(space < spaces - 1)
    def _():
        pl.semaphore_signal(barrier, inc=1, device_id={"space": space + 1}, device_id_type=MESH)

    for fetch in fetches:
        fetch.start()

    row_id = lax.broadcasted_iota(jnp.int32, (NO, NO), 0)
    col_id = lax.broadcasted_iota(jnp.int32, (NO, NO), 1)
    original = 2 * (row_id % NE) + row_id // NE
    select = col_id == original
    permute = jnp.where(select, F32(1), F32(0)).astype(BF16)
    diagonal = jnp.where(select, F32(1), F32(0))

    def prior(b):
        return jnp.concatenate([pl_ref[b], pg_ref[b]], axis=0)

    def make_bare(b):
        wide = jnp.concatenate([pl_ref[b], pg_ref[b]], axis=1)
        half = dot(g_ref[b], wide).astype(BF16)
        bare[b] = dot_t(stacked(half), g_ref[b]).astype(BF16)

    def rise(b):
        return stacked(dot(ct[b], side_by_side(bare[b])).astype(BF16))

    for g in range(2):
        recvs[g][0:PAD] = jnp.zeros((PAD, 16, NO), BF16)
        recvs[g][PAD + NE :] = jnp.zeros((PAD, 16, NO), BF16)
    for fetch in fetches:
        fetch.wait()
    for b in range(NB):
        ct[b] = c_ref[b].T
        mixed[b] = dot(permute, g_ref[b]).astype(BF16)

    make_bare(0)
    make_bare(NB - 1)
    up_out[...] = dot(rise(NB - 1), c_ref[NB - 1]).astype(BF16)

    open_count = active_ref[me]
    lane8 = lax.broadcasted_iota(jnp.int32, (8, NO), 1)
    sub8 = lax.broadcasted_iota(jnp.int32, (8, NO), 0)

    def finish(blocks, ldos):
        for b in blocks:
            fall = stacked(dot(c_ref[b], side_by_side(bare[b + 1])).astype(BF16))
            if b == 0:
                left[0, :, :NO] = fall
            else:
                left[b] = jnp.concatenate([rise(b - 1), fall], axis=1)
        for b in blocks:
            if b == 0:
                hops = dot(left[0, :, :NO], ct[0]) + up_in[...].astype(F32)
            else:
                hops = dot(left[b], jnp.concatenate([c_ref[b - 1], ct[b]], axis=0))
            source[b] = side_by_side((prior(b).astype(F32) + hops).astype(BF16))
        for b in blocks:
            half[b] = stacked(dot(mixed[b], source[b]).astype(BF16))
        for b in blocks:
            result = dot_t(half[b], g_ref[b])
            result = result * jnp.where(space * NB + b < open_count, F32(1), F32(0))
            trace = jnp.sum((result[:NO] + result[NO:]) * diagonal, axis=0, keepdims=True)
            g, inside = int(b in (1, 2, 3, 4)), b % HALF
            for kind in range(2):
                for r in range(2):
                    begin = kind * 8 + inside * 2 + r
                    at = kind * NO + r * NE
                    rows[g, pl.ds(begin, NE, stride=16), :] = result[at : at + NE]
            ldos = jnp.where(sub8 == b, jnp.broadcast_to(trace, (8, NO)), ldos)
        return ldos

    def exchange(g, p):
        return pltpu.make_async_remote_copy(
            src_ref=send.at[g, p], dst_ref=recvs[g].at[PAD + me], send_sem=x_send.at[g], recv_sem=x_recv.at[g],
            device_id=(p, space), device_id_type=MESH,
        )

    def pack(g):
        send[g] = rows[g].reshape(NE, 16, NO).astype(BF16)

    def start(g, targets):
        for p in targets:
            exchange(g, p).start()

    def whole(g):
        return pltpu.make_async_remote_copy(
            src_ref=send.at[g, pl.ds(0, NE - 1)], dst_ref=recvs[g].at[pl.ds(0, NE - 1)],
            send_sem=x_send.at[g], recv_sem=x_recv.at[g],
            device_id={"energy": (me + 1) % NE}, device_id_type=MESH,
        )

    ldos = jnp.zeros((8, NO), F32)
    for b in range(1, NB - 1):
        make_bare(b)
    @pl.when(space == 0)
    def _():
        up_in[...] = jnp.zeros_like(up_in)

    @pl.when(space == spaces - 1)
    def _():
        bare[NB] = jnp.zeros((2 * NO, NO), BF16)

    ldos = finish((1, 2, 3, 4), ldos)
    pack(1)

    neighbours = (space > 0).astype(jnp.int32) + (space < spaces - 1).astype(jnp.int32)
    pl.semaphore_wait(barrier, NE - 1 + neighbours)

    down_copy = pltpu.make_async_remote_copy(
        src_ref=bare.at[0], dst_ref=bare.at[NB], send_sem=halo_send.at[0], recv_sem=halo_recv.at[0],
        device_id={"space": lax.rem(space + spaces - 1, spaces)}, device_id_type=MESH,
    )
    up_copy = pltpu.make_async_remote_copy(
        src_ref=up_out, dst_ref=up_in, send_sem=halo_send.at[1], recv_sem=halo_recv.at[1],
        device_id={"space": lax.rem(space + 1, spaces)}, device_id_type=MESH,
    )

    @pl.when(space > 0)
    def _():
        down_copy.start()

    @pl.when(space < spaces - 1)
    def _():
        up_copy.start()

    start(1, peers)

    @pl.when(space < spaces - 1)
    def _():
        down_copy.wait_recv()


    @pl.when(space > 0)
    def _():
        up_copy.wait_recv()

    ldos = finish((5, 6, 7, 0), ldos)
    pack(0)
    start(0, peers)
    for g in range(2):
        recvs[g][PAD + me] = send[g, me]

    def as_row(columns):
        sums = jnp.sum(columns, axis=1, keepdims=True)
        return jnp.sum(jnp.where(lane8 == sub8, sums, F32(0)), axis=0, keepdims=True)[:, :NB]

    ldos_ref[...] = as_row(ldos) / NO

    occupied = F32(phonon_occupation)
    coupling8 = jnp.where(sub8 % 2 == 0, pc_ref[0:1, :], pc_ref[1:2, :])
    strong, weak = coupling8 * (1 + occupied), coupling8 * occupied
    s0, s1 = shift_ref[0], shift_ref[1]

    first = sub8 < 2
    place1 = jnp.where(first, sub8 + 8, sub8)
    place0 = jnp.where(first, sub8, sub8 + 8)

    def sigma(g):
        whole(g).wait_recv()
        recv = recvs[g]

        def step(e, carry):
            at = PAD + e
            here = recv[at].astype(F32)
            up = recv[at + s0].astype(F32) + recv[at + s1].astype(F32)
            down = recv[at - s0].astype(F32) + recv[at - s1].astype(F32)
            less = (strong * up[:8] + weak * down[:8]).astype(BF16).astype(F32)
            great = (strong * down[8:] + weak * up[8:]).astype(BF16).astype(F32)
            early[g, 0, e] = less
            early[g, 1, e] = great
            flow = less * here[8:] - great * here[:8]
            sums = jnp.where(lane8 == (place1 if g == 1 else place0), jnp.sum(flow, axis=1, keepdims=True), F32(0))
            if g == 1:
                part[e] = sums
            else:
                flows[e] = jnp.sum(part[e] + sums, axis=0, keepdims=True)
            return carry

        lax.fori_loop(0, NE, step, 0, unroll=32)

    sigma(1)
    sigma(0)

    def share(p):
        return pltpu.make_async_remote_copy(
            src_ref=flows.at[p], dst_ref=total.at[me], send_sem=t_send, recv_sem=t_recv,
            device_id=(p, space), device_id_type=MESH,
        )

    for p in peers:
        share(p).start()
    total[me] = flows[me]

    def merge(e, carry):
        for kind, out in enumerate((sl_ref, sg_ref)):
            low = jnp.where(first, early[0, kind, e], early[1, kind, e])
            high = jnp.where(first, early[1, kind, e], early[0, kind, e])
            out[e] = jnp.concatenate([low, high], axis=0).astype(BF16)
        return carry

    lax.fori_loop(0, NE, merge, 0, unroll=8)
    shares = pltpu.make_async_remote_copy(
        src_ref=flows.at[pl.ds(0, NE - 1)], dst_ref=total.at[pl.ds(0, NE - 1)], send_sem=t_send, recv_sem=t_recv,
        device_id=(peers[0], space), device_id_type=MESH,
    )
    shares.wait_recv()
    lanes = [total[e] for e in range(NE)]
    while len(lanes) > 1:
        lanes = [one + other for one, other in zip(lanes[::2], lanes[1::2])]
    cur_ref[...] = as_row(jnp.where(lane8 // 2 == sub8, jnp.broadcast_to(lanes[0], (8, NO)), F32(0))) / NO
    shares.wait_send()

    @pl.when(space > 0)
    def _():
        down_copy.wait_send()

    @pl.when(space < spaces - 1)
    def _():
        up_copy.wait_send()

    whole(1).wait_send()
    whole(0).wait_send()


def keep(*refs):
    copies = []
    for i in range(2):
        for n in range(CUTS):
            piece = pl.ds(n * (NE // CUTS), NE // CUTS)
            copies.append(pltpu.make_async_copy(refs[i].at[piece], refs[4 + i].at[piece], refs[8].at[4 + CUTS * i + n]))
    copies += [pltpu.make_async_copy(refs[i], refs[4 + i], refs[8].at[i]) for i in (2, 3)]
    for copy in copies:
        copy.start()
    for copy in copies:
        copy.wait()


def local(
    green_ret, prior_less, prior_great, coupling, phonon_coupling, phonon_shift, active_blocks
):
    vmem = pl.BlockSpec(memory_space=pltpu.VMEM)
    hbm = pl.BlockSpec(memory_space=pltpu.HBM)
    dma = pltpu.SemaphoreType.DMA
    sigma_l, sigma_g, current, ldos = pl.pallas_call(
        kernel,
        out_shape=(
            jax.ShapeDtypeStruct((NE, 2 * NB, NO), BF16),
            jax.ShapeDtypeStruct((NE, 2 * NB, NO), BF16),
            jax.ShapeDtypeStruct((1, NB), F32),
            jax.ShapeDtypeStruct((1, NB), F32),
        ),
        in_specs=[hbm] * 7,
        out_specs=[vmem] * 4,
        scratch_shapes=[
            pltpu.VMEM((NB, NO, NO), BF16),
            pltpu.VMEM((NB, NO, NO), BF16),
            pltpu.VMEM((NB, NO, NO), BF16),
            pltpu.VMEM((NB, NO, NO), BF16),
            pltpu.VMEM((2, NO), F32),
            pltpu.SMEM((2,), jnp.int32),
            pltpu.SMEM((NE,), jnp.int32),
            dma((7,)),
            pltpu.VMEM((NB, 2 * NO, 2 * NO), BF16),
            pltpu.VMEM((NB, NO, 2 * NO), BF16),
            pltpu.VMEM((NB, 2 * NO, NO), BF16),
            pltpu.VMEM((NB, NO, NO), BF16),
            pltpu.VMEM((NB + 1, 2 * NO, NO), BF16),
            pltpu.VMEM((NB, NO, NO), BF16),
            pltpu.VMEM((2 * NO, NO), BF16),
            pltpu.VMEM((2 * NO, NO), BF16),
            pltpu.VMEM((2, NE * 16, NO), F32),
            pltpu.VMEM((2, NE, 16, NO), BF16),
            pltpu.VMEM((NE + 2 * PAD, 16, NO), BF16),
            pltpu.VMEM((NE + 2 * PAD, 16, NO), BF16),
            pltpu.VMEM((2, 2, NE, 8, NO), F32),
            pltpu.VMEM((NE, 8, NO), F32),
            pltpu.VMEM((NE, 1, NO), F32),
            pltpu.VMEM((NE, 1, NO), F32),
            dma((2,)), dma((2,)), dma((2,)), dma((2,)), dma, dma,
        ],
        compiler_params=pltpu.CompilerParams(
            collective_id=0, has_side_effects=True, vmem_limit_bytes=32 << 20
        ),
        name="born_step",
    )(
        *(
            pltpu.with_memory_space_constraint(operand, pltpu.HBM)
            for operand in (
                green_ret.reshape(NB, NO, NO),
                prior_less.reshape(NB, NO, NO),
                prior_great.reshape(NB, NO, NO),
                coupling,
                phonon_coupling,
                phonon_shift,
                active_blocks,
            )
        )
    )
    results = (sigma_l, sigma_g, current, ldos)
    sigma_l, sigma_g, current, ldos = pl.pallas_call(
        keep,
        out_shape=tuple(jax.ShapeDtypeStruct(r.shape, r.dtype) for r in results),
        in_specs=[vmem] * 4,
        out_specs=[hbm] * 4,
        scratch_shapes=[dma((4 + 2 * CUTS,))],
        name="keep",
    )(*(pltpu.with_memory_space_constraint(r, pltpu.VMEM) for r in results))
    shape = (NE, NB, 2, NO)
    return sigma_l.reshape(shape), sigma_g.reshape(shape), current, ldos


def solution(mesh):
    return jax.shard_map(
        local,
        mesh=mesh,
        in_specs=(
            P("energy", "space", None, None),
            P("energy", "space", None, None),
            P("energy", "space", None, None),
            P("space", None, None),
            P("energy", None),
            P(),
            P(),
        ),
        out_specs=(
            P(None, "space", "energy", None),
            P(None, "space", "energy", None),
            P("energy", "space"),
            P("energy", "space"),
        ),
        check_vma=False,
    )
```

```python
import functools

import jax
import jax.numpy as jnp
from jax import lax
from jax.experimental import pallas as pl
from jax.experimental.pallas import tpu as pltpu
from jax.sharding import PartitionSpec as P

phonon_occupation = 0.5
MESH = pl.DeviceIdType.MESH
F32 = jnp.float32
BF16 = jnp.bfloat16

NE = 64
NB = 8
NO = 128
HALF = 4
PAD = 32
CUTS = 2
SIDE = 8


def dot(left, right):
    return jnp.dot(left, right, preferred_element_type=F32)


def dot_t(left, right):
    return lax.dot_general(left, right, (((1,), (1,)), ((), ())), preferred_element_type=F32)


def side_by_side(stacked):
    return jnp.concatenate([stacked[:NO], stacked[NO:]], axis=1)


def stacked(wide):
    return jnp.concatenate([wide[:, :NO], wide[:, NO:]], axis=0)


def kernel(
    g_hbm, pl_hbm, pg_hbm, c_hbm, pc_hbm, shift_hbm, active_hbm,
    sl_ref, sg_ref, cur_ref, ldos_ref,
    g_ref, pl_ref, pg_ref, c_ref, pc_ref, shift_ref, active_ref, in_sem,
    left, source, half, mixed, bare, ct, up_out, up_in, rows, send, recv_low, recv_high, early, part, flows, total,
    halo_send, halo_recv, x_send, x_recv, t_send, t_recv,
):
    me = lax.axis_index("energy")
    space = lax.axis_index("space")
    spaces = lax.axis_size("space")
    recvs = (recv_low, recv_high)

    fetches = [
        pltpu.make_async_copy(source, target, in_sem.at[i])
        for i, (source, target) in enumerate((
            (g_hbm, g_ref), (pl_hbm, pl_ref), (pg_hbm, pg_ref), (c_hbm, c_ref),
            (pc_hbm, pc_ref), (shift_hbm, shift_ref), (active_hbm, active_ref),
        ))
    ]

    z, y = me // SIDE, me % SIDE
    in_y = [lax.rem(y + k, SIDE) for k in range(SIDE)]
    in_z = [lax.rem(z + k, SIDE) * SIDE for k in range(SIDE)]
    steps = (1, 7, 2, 6, 3, 5, 4, 0)
    offsets = [(dy, (dy + j) % SIDE) for j in (4, 0, 2, 6, 1, 5, 3, 7) for dy in steps if j or dy]
    offsets.sort(key=lambda at: -sum(min(d, SIDE - d) for d in at))
    peers = [in_z[dz] + in_y[dy] for dy, dz in offsets]

    barrier = pltpu.get_barrier_semaphore()

    for p in peers:
        pl.semaphore_signal(barrier, inc=1, device_id=(p, space), device_id_type=MESH)

    @pl.when(space > 0)
    def _():
        pl.semaphore_signal(barrier, inc=1, device_id={"space": space - 1}, device_id_type=MESH)

    @pl.when(space < spaces - 1)
    def _():
        pl.semaphore_signal(barrier, inc=1, device_id={"space": space + 1}, device_id_type=MESH)

    for fetch in fetches:
        fetch.start()

    row_id = lax.broadcasted_iota(jnp.int32, (NO, NO), 0)
    col_id = lax.broadcasted_iota(jnp.int32, (NO, NO), 1)
    original = 2 * (row_id % NE) + row_id // NE
    select = col_id == original
    permute = jnp.where(select, F32(1), F32(0)).astype(BF16)
    diagonal = jnp.where(select, F32(1), F32(0))

    def prior(b):
        return jnp.concatenate([pl_ref[b], pg_ref[b]], axis=0)

    def make_bare(b):
        wide = jnp.concatenate([pl_ref[b], pg_ref[b]], axis=1)
        half = dot(g_ref[b], wide).astype(BF16)
        bare[b] = dot_t(stacked(half), g_ref[b]).astype(BF16)

    def rise(b):
        return stacked(dot(ct[b], side_by_side(bare[b])).astype(BF16))

    for g in range(2):
        recvs[g][0:PAD] = jnp.zeros((PAD, 16, NO), BF16)
        recvs[g][PAD + NE :] = jnp.zeros((PAD, 16, NO), BF16)
    for fetch in fetches:
        fetch.wait()
    for b in range(NB):
        ct[b] = c_ref[b].T
        mixed[b] = dot(permute, g_ref[b]).astype(BF16)

    make_bare(0)
    make_bare(NB - 1)
    up_out[...] = dot(rise(NB - 1), c_ref[NB - 1]).astype(BF16)

    open_count = active_ref[me]
    lane8 = lax.broadcasted_iota(jnp.int32, (8, NO), 1)
    sub8 = lax.broadcasted_iota(jnp.int32, (8, NO), 0)

    def finish(blocks, ldos):
        for b in blocks:
            fall = stacked(dot(c_ref[b], side_by_side(bare[b + 1])).astype(BF16))
            if b == 0:
                left[0, :, :NO] = fall
            else:
                left[b] = jnp.concatenate([rise(b - 1), fall], axis=1)
        for b in blocks:
            if b == 0:
                hops = dot(left[0, :, :NO], ct[0]) + up_in[...].astype(F32)
            else:
                hops = dot(left[b], jnp.concatenate([c_ref[b - 1], ct[b]], axis=0))
            source[b] = side_by_side((prior(b).astype(F32) + hops).astype(BF16))
        for b in blocks:
            half[b] = stacked(dot(mixed[b], source[b]).astype(BF16))
        for b in blocks:
            result = dot_t(half[b], g_ref[b])
            result = result * jnp.where(space * NB + b < open_count, F32(1), F32(0))
            trace = jnp.sum((result[:NO] + result[NO:]) * diagonal, axis=0, keepdims=True)
            g, inside = int(b in (1, 2, 3, 4)), b % HALF
            for kind in range(2):
                for r in range(2):
                    begin = kind * 8 + inside * 2 + r
                    at = kind * NO + r * NE
                    rows[g, pl.ds(begin, NE, stride=16), :] = result[at : at + NE]
            ldos = jnp.where(sub8 == b, jnp.broadcast_to(trace, (8, NO)), ldos)
        return ldos

    def exchange(g, p):
        return pltpu.make_async_remote_copy(
            src_ref=send.at[g, p], dst_ref=recvs[g].at[PAD + me], send_sem=x_send.at[g], recv_sem=x_recv.at[g],
            device_id=(p, space), device_id_type=MESH,
        )

    def pack(g):
        send[g] = rows[g].reshape(NE, 16, NO).astype(BF16)

    def start(g, targets):
        for p in targets:
            exchange(g, p).start()

    def whole(g):
        return pltpu.make_async_remote_copy(
            src_ref=send.at[g, pl.ds(0, NE - 1)], dst_ref=recvs[g].at[pl.ds(0, NE - 1)],
            send_sem=x_send.at[g], recv_sem=x_recv.at[g],
            device_id={"energy": (me + 1) % NE}, device_id_type=MESH,
        )

    ldos = jnp.zeros((8, NO), F32)
    for b in range(1, NB - 1):
        make_bare(b)
    @pl.when(space == 0)
    def _():
        up_in[...] = jnp.zeros_like(up_in)

    @pl.when(space == spaces - 1)
    def _():
        bare[NB] = jnp.zeros((2 * NO, NO), BF16)

    ldos = finish((1, 2, 3, 4), ldos)
    pack(1)

    neighbours = (space > 0).astype(jnp.int32) + (space < spaces - 1).astype(jnp.int32)
    pl.semaphore_wait(barrier, NE - 1 + neighbours)

    down_copy = pltpu.make_async_remote_copy(
        src_ref=bare.at[0], dst_ref=bare.at[NB], send_sem=halo_send.at[0], recv_sem=halo_recv.at[0],
        device_id={"space": lax.rem(space + spaces - 1, spaces)}, device_id_type=MESH,
    )
    up_copy = pltpu.make_async_remote_copy(
        src_ref=up_out, dst_ref=up_in, send_sem=halo_send.at[1], recv_sem=halo_recv.at[1],
        device_id={"space": lax.rem(space + 1, spaces)}, device_id_type=MESH,
    )

    @pl.when(space > 0)
    def _():
        down_copy.start()

    @pl.when(space < spaces - 1)
    def _():
        up_copy.start()

    start(1, peers)

    @pl.when(space < spaces - 1)
    def _():
        down_copy.wait_recv()


    @pl.when(space > 0)
    def _():
        up_copy.wait_recv()

    ldos = finish((5, 6, 7, 0), ldos)
    pack(0)
    start(0, peers)
    for g in range(2):
        recvs[g][PAD + me] = send[g, me]

    def as_row(columns):
        sums = jnp.sum(columns, axis=1, keepdims=True)
        return jnp.sum(jnp.where(lane8 == sub8, sums, F32(0)), axis=0, keepdims=True)[:, :NB]

    ldos_ref[...] = as_row(ldos) / NO

    occupied = F32(phonon_occupation)
    coupling8 = jnp.where(sub8 % 2 == 0, pc_ref[0:1, :], pc_ref[1:2, :])
    strong, weak = coupling8 * (1 + occupied), coupling8 * occupied
    s0, s1 = shift_ref[0], shift_ref[1]

    first = sub8 < 2
    place1 = jnp.where(first, sub8 + 8, sub8)
    place0 = jnp.where(first, sub8, sub8 + 8)

    def sigma(g):
        whole(g).wait_recv()
        recv = recvs[g]

        def step(e, carry):
            at = PAD + e
            here = recv[at].astype(F32)
            up = recv[at + s0].astype(F32) + recv[at + s1].astype(F32)
            down = recv[at - s0].astype(F32) + recv[at - s1].astype(F32)
            less = (strong * up[:8] + weak * down[:8]).astype(BF16).astype(F32)
            great = (strong * down[8:] + weak * up[8:]).astype(BF16).astype(F32)
            early[g, 0, e] = less
            early[g, 1, e] = great
            flow = less * here[8:] - great * here[:8]
            sums = jnp.where(lane8 == (place1 if g == 1 else place0), jnp.sum(flow, axis=1, keepdims=True), F32(0))
            if g == 1:
                part[e] = sums
            else:
                flows[e] = jnp.sum(part[e] + sums, axis=0, keepdims=True)
            return carry

        lax.fori_loop(0, NE, step, 0, unroll=64)

    sigma(1)
    sigma(0)

    def share(p):
        return pltpu.make_async_remote_copy(
            src_ref=flows.at[p], dst_ref=total.at[me], send_sem=t_send, recv_sem=t_recv,
            device_id=(p, space), device_id_type=MESH,
        )

    for p in peers:
        share(p).start()
    total[me] = flows[me]

    def merge(e, carry):
        for kind, out in enumerate((sl_ref, sg_ref)):
            low = jnp.where(first, early[0, kind, e], early[1, kind, e])
            high = jnp.where(first, early[1, kind, e], early[0, kind, e])
            out[e] = jnp.concatenate([low, high], axis=0).astype(BF16)
        return carry

    lax.fori_loop(0, NE, merge, 0, unroll=8)
    shares = pltpu.make_async_remote_copy(
        src_ref=flows.at[pl.ds(0, NE - 1)], dst_ref=total.at[pl.ds(0, NE - 1)], send_sem=t_send, recv_sem=t_recv,
        device_id=(peers[0], space), device_id_type=MESH,
    )
    shares.wait_recv()
    lanes = [total[e] for e in range(NE)]
    while len(lanes) > 1:
        lanes = [one + other for one, other in zip(lanes[::2], lanes[1::2])]
    cur_ref[...] = as_row(jnp.where(lane8 // 2 == sub8, jnp.broadcast_to(lanes[0], (8, NO)), F32(0))) / NO
    shares.wait_send()

    @pl.when(space > 0)
    def _():
        down_copy.wait_send()

    @pl.when(space < spaces - 1)
    def _():
        up_copy.wait_send()

    whole(1).wait_send()
    whole(0).wait_send()


def keep(*refs):
    copies = []
    for i in range(2):
        for n in range(CUTS):
            piece = pl.ds(n * (NE // CUTS), NE // CUTS)
            copies.append(pltpu.make_async_copy(refs[i].at[piece], refs[4 + i].at[piece], refs[8].at[4 + CUTS * i + n]))
    copies += [pltpu.make_async_copy(refs[i], refs[4 + i], refs[8].at[i]) for i in (2, 3)]
    for copy in copies:
        copy.start()
    for copy in copies:
        copy.wait()


def local(
    green_ret, prior_less, prior_great, coupling, phonon_coupling, phonon_shift, active_blocks
):
    vmem = pl.BlockSpec(memory_space=pltpu.VMEM)
    hbm = pl.BlockSpec(memory_space=pltpu.HBM)
    dma = pltpu.SemaphoreType.DMA
    sigma_l, sigma_g, current, ldos = pl.pallas_call(
        kernel,
        out_shape=(
            jax.ShapeDtypeStruct((NE, 2 * NB, NO), BF16),
            jax.ShapeDtypeStruct((NE, 2 * NB, NO), BF16),
            jax.ShapeDtypeStruct((1, NB), F32),
            jax.ShapeDtypeStruct((1, NB), F32),
        ),
        in_specs=[hbm] * 7,
        out_specs=[vmem] * 4,
        scratch_shapes=[
            pltpu.VMEM((NB, NO, NO), BF16),
            pltpu.VMEM((NB, NO, NO), BF16),
            pltpu.VMEM((NB, NO, NO), BF16),
            pltpu.VMEM((NB, NO, NO), BF16),
            pltpu.VMEM((2, NO), F32),
            pltpu.SMEM((2,), jnp.int32),
            pltpu.SMEM((NE,), jnp.int32),
            dma((7,)),
            pltpu.VMEM((NB, 2 * NO, 2 * NO), BF16),
            pltpu.VMEM((NB, NO, 2 * NO), BF16),
            pltpu.VMEM((NB, 2 * NO, NO), BF16),
            pltpu.VMEM((NB, NO, NO), BF16),
            pltpu.VMEM((NB + 1, 2 * NO, NO), BF16),
            pltpu.VMEM((NB, NO, NO), BF16),
            pltpu.VMEM((2 * NO, NO), BF16),
            pltpu.VMEM((2 * NO, NO), BF16),
            pltpu.VMEM((2, NE * 16, NO), F32),
            pltpu.VMEM((2, NE, 16, NO), BF16),
            pltpu.VMEM((NE + 2 * PAD, 16, NO), BF16),
            pltpu.VMEM((NE + 2 * PAD, 16, NO), BF16),
            pltpu.VMEM((2, 2, NE, 8, NO), F32),
            pltpu.VMEM((NE, 8, NO), F32),
            pltpu.VMEM((NE, 1, NO), F32),
            pltpu.VMEM((NE, 1, NO), F32),
            dma((2,)), dma((2,)), dma((2,)), dma((2,)), dma, dma,
        ],
        compiler_params=pltpu.CompilerParams(
            collective_id=0, has_side_effects=True, vmem_limit_bytes=32 << 20
        ),
        name="born_step",
    )(
        *(
            pltpu.with_memory_space_constraint(operand, pltpu.HBM)
            for operand in (
                green_ret.reshape(NB, NO, NO),
                prior_less.reshape(NB, NO, NO),
                prior_great.reshape(NB, NO, NO),
                coupling,
                phonon_coupling,
                phonon_shift,
                active_blocks,
            )
        )
    )
    results = (sigma_l, sigma_g, current, ldos)
    sigma_l, sigma_g, current, ldos = pl.pallas_call(
        keep,
        out_shape=tuple(jax.ShapeDtypeStruct(r.shape, r.dtype) for r in results),
        in_specs=[vmem] * 4,
        out_specs=[hbm] * 4,
        scratch_shapes=[dma((4 + 2 * CUTS,))],
        name="keep",
    )(*(pltpu.with_memory_space_constraint(r, pltpu.VMEM) for r in results))
    shape = (NE, NB, 2, NO)
    return sigma_l.reshape(shape), sigma_g.reshape(shape), current, ldos


def solution(mesh):
    return jax.shard_map(
        local,
        mesh=mesh,
        in_specs=(
            P("energy", "space", None, None),
            P("energy", "space", None, None),
            P("energy", "space", None, None),
            P("space", None, None),
            P("energy", None),
            P(),
            P(),
        ),
        out_specs=(
            P(None, "space", "energy", None),
            P(None, "space", "energy", None),
            P("energy", "space"),
            P("energy", "space"),
        ),
        check_vma=False,
    )
```
